512 devices in a mesh: context: 128 (over z_hi, x, y, core), chan: 4 (over z_lo).
Axes of the slice: x: 4, y: 8, z: 8 (z_hi: 2, z_lo: 4; z = z_hi * 4 + z_lo), core: 2. Of those that a mesh axis runs over, the one named last changes fastest.
Arguments:
- signal: float32 [64, 131072], P('chan', 'context'), may hold values from -6 to 6
- filter_taps: float32 [131072], P('context'), may hold values from -6 to 6
- skip_gain: float32 [64], P('chan'), may hold values from 0.5 to 1.5
- cotangent: float32 [64, 131072], P('chan', 'context'), may hold values from -6 to 6
Outputs:
- output: float32 [64, 131072], P('chan', 'context')
- grad_signal: float32 [64, 131072], P('chan', 'context')
- grad_filter: float32 [131072], P('context')
The draws below stay inside these ranges and needn't reach their ends.
All inputs are finite; a program needn't handle non-finite values.
Results may differ from the reference program's by a relative error of at most 0.00013.
Values sent between devices are 32-bit elements; how exact they have to be, the bound alone decides.
A program may use at most 64 MiB of HBM per device.

```python
import math
import jax
import jax.numpy as jnp
from jax import lax

CH = 64
SEQ = 131072


def level_of(rng, extent, cuts, smallest, top_value):
    level, own = 1.0, jax.random.fold_in(rng, 6)
    for axis_at, shards_of in cuts:
        steps = jnp.exp(jax.random.uniform(jax.random.fold_in(own, axis_at), (shards_of,), jnp.float32, smallest / len(cuts), top_value / len(cuts)))
        level = level * jnp.repeat(steps, extent[axis_at] // shards_of).reshape([-1 if axis == axis_at else 1 for axis in range(len(extent))])
    return level


def scatter_about(stream_key, dims, deviation, bound, split=(), kind=jnp.bfloat16):
    loudness = level_of(stream_key, dims, split, -0.22, 0.18) if split else 1.0
    values = jax.random.normal(stream_key, dims, jnp.float32) * deviation * loudness
    return jnp.minimum(jnp.maximum(values, -bound), bound).astype(kind)


def setup_inputs(seed: int = 0) -> dict:
    key_list = jax.random.split(jax.random.key(seed), 5)
    return {
        "signal": scatter_about(key_list[0], (CH, SEQ), 1.0, 6.0, ((0, 4), (1, 128)), jnp.float32),
        "filter_taps": scatter_about(key_list[1], (SEQ,), 1.0, 6.0, ((0, 128),), jnp.float32),
        "skip_gain": jnp.clip(0.5 + 1.0 * jax.random.uniform(key_list[2], (CH,), jnp.float32) ** level_of(key_list[2], (CH,), ((0, 4),), -0.2, 0.2), 0.5, 1.5),
        "cotangent": scatter_about(key_list[3], (CH, SEQ), 1.0, 6.0, ((0, 4), (1, 128)), jnp.float32),
    }


def reference(signal, filter_taps, skip_gain, cotangent):
    period = 2 * SEQ
    factor = 1.0 / math.sqrt(SEQ)
    spec_signal = jnp.fft.rfft(signal, n=period, axis=-1)
    spec_filter = jnp.fft.rfft(filter_taps, n=period)
    spec_cot = jnp.fft.rfft(cotangent, n=period, axis=-1)
    conv = jnp.fft.irfft(spec_signal * spec_filter[None, :], n=period, axis=-1)[:, :SEQ]
    output = (conv * factor + skip_gain[:, None] * signal).astype(jnp.float32)
    back = jnp.fft.irfft(spec_cot * jnp.conj(spec_filter)[None, :], n=period, axis=-1)[:, :SEQ]
    grad_signal = (back * factor + skip_gain[:, None] * cotangent).astype(jnp.float32)
    summed = lax.optimization_barrier(jnp.sum(spec_cot * jnp.conj(spec_signal), axis=0))
    grad_filter = (jnp.fft.irfft(summed, n=period)[:SEQ] * factor).astype(jnp.float32)
    return (output, grad_signal, grad_filter)
```

```python
import functools
import math

import jax
import jax.numpy as jnp
import numpy as np
from jax import lax
from jax.experimental import pallas as pl
from jax.experimental.pallas import tpu as pltpu
from jax.sharding import PartitionSpec as P

MESH = pl.DeviceIdType.MESH
F32, BF16 = jnp.float32, jnp.bfloat16
BLOCKS, CHANS = 128, 4
A, T = 8, 128
LOCAL = A * T
PAD = 2 * BLOCKS
ROWS = 32
SCALE = 1.0 / (PAD * LOCAL * math.sqrt(BLOCKS * LOCAL))


def as_real(left):
    return np.block([[left.real, -left.imag], [left.imag, left.real]])


def halves(table):
    high = np.asarray(table, np.float32).astype(BF16)
    low = (table - high.astype(np.float64)).astype(np.float32).astype(BF16)
    return np.stack([high, low])


def tables():
    turn = lambda x: np.exp(-2j * np.pi * x)
    t = np.arange(T)
    ka = np.arange(A)
    near = turn(np.outer(t, t) / T)
    far = turn(np.outer(np.arange(PAD), np.arange(BLOCKS)) / PAD)
    fold = 1 + 1j * turn(np.arange(PAD) / PAD)
    back = far.conj().T
    fore = as_real(near)
    last = as_real(near.conj()).T
    spread = np.zeros((2, 128, A * ROWS))
    gather = np.zeros((A * ROWS, 128))
    for k in range(A):
        spread[:, k, k * ROWS : (k + 1) * ROWS] = 1
        spread[1, k, k * ROWS + ROWS // 2 : (k + 1) * ROWS] = -1
        gather[k * ROWS + ROWS // 2 : (k + 1) * ROWS, k] = 1
    twist = turn(np.outer(4 * ka + 1, t) / (4 * LOCAL))
    small = np.zeros((4, A, 128))
    roots = turn(np.outer(ka, 4 * ka + 1) / 32)
    for i, part in enumerate((roots.real, roots.imag, roots.real.T, roots.imag.T)):
        small[i, :, :A] = part
    return dict(
        fore=halves(fore),
        last=halves(last),
        wide=halves(as_real(far)),
        wide_f=halves(as_real(far * fold[:, None])),
        narrow=halves(as_real(back)),
        narrow_g=halves(as_real(back * fold.conj()[None, :])),
        spread=spread.astype(BF16),
        gather=gather.astype(BF16),
        twist=np.stack([twist.real, twist.imag]).astype(np.float32),
        small=small.astype(np.float32),
    )


ROOT = [[complex(np.exp(-2j * np.pi * a * (4 * k + 1) / 32)) for k in range(A)] for a in range(A)]


def split(x):
    high = x.astype(BF16)
    return high, (x - high.astype(F32)).astype(BF16)


def dot(x, y, dims):
    return lax.dot_general(x, y, (dims, ((), ())), preferred_element_type=F32)


NN = ((1,), (0,))
NT = ((1,), (1,))


def product(left, right, dims=NN):
    (lh, ll), (rh, rl) = left, right
    return dot(lh, rh, dims) + (dot(lh, rl, dims) + dot(ll, rh, dims))


def local_forward(signal, cotangent, taps, twist, small, fore):
    parts = []
    for k in range(A):
        re = im = None
        for a in range(A):
            x = jnp.concatenate([signal(a), cotangent(a)], axis=0)
            c = ROOT[a][k]
            re = x * c.real if re is None else re + x * c.real
            im = x * c.imag if im is None else im + x * c.imag
        wr, wi = twist[0][k : k + 1], twist[1][k : k + 1]
        parts.append(jnp.concatenate([re * wr - im * wi, re * wi + im * wr], axis=1))
    z = split(jnp.concatenate(parts, axis=0))
    out = product(fore, z, NT)
    re = im = 0.0
    for a in range(A):
        x = taps[a : a + 1]
        re = re + small[2][:, a : a + 1] * x
        im = im + small[3][:, a : a + 1] * x
    wr, wi = twist
    re, im = re * wr - im * wi, re * wi + im * wr
    zf = jnp.concatenate(
        [
            jnp.concatenate([re, im], axis=1),
            jnp.concatenate([im, -re], axis=1),
            jnp.zeros((128 - 2 * A, 2 * T), F32),
        ],
        axis=0,
    )
    outf = product((fore[0][:T], fore[1][:T]), split(zf), NT)
    return [out[:T, :128], out[:T, 128:], out[T:, :128], out[T:, 128:], outf]


def middle(rows, wide, wide_f, narrow, narrow_g, spread, gather):
    x = jnp.concatenate(
        [jnp.concatenate(rows[0:2], axis=1), jnp.concatenate(rows[2:4], axis=1)], axis=0
    )
    v = product(wide, split(x))
    xf = rows[4]
    xf = jnp.concatenate([xf, pltpu.roll(xf, 128 - A, 1)], axis=0)
    g = product(wide_f, split(xf))
    gh, gl = split(g)
    gr = dot(gh[:PAD], spread[0], NN) + dot(gl[:PAD], spread[0], NN)
    gi = dot(gh[PAD:], spread[1], NN) + dot(gl[PAD:], spread[1], NN)
    vr, vi = v[:PAD], v[PAD:]
    p = jnp.concatenate([vr * gr - vi * gi, vr * gi + vi * gr], axis=0)
    w = product(narrow, split(p))
    turned = jnp.concatenate(
        [pltpu.roll(v[:, :128], ROWS // 2, 1), pltpu.roll(v[:, 128:], ROWS // 2, 1)], axis=1
    )
    sr, si = turned[:PAD], turned[PAD:]
    qh, ql = split(jnp.concatenate([vr * sr + vi * si, vi * sr - vr * si], axis=0))
    d = dot(qh, gather, NN) + dot(ql, gather, NN)
    e = product(narrow_g, split(d))
    grad = e[:BLOCKS] + pltpu.roll(e[BLOCKS:], A, 1)
    return [w[:BLOCKS, :128], w[:BLOCKS, 128:], w[BLOCKS:, :128], w[BLOCKS:, 128:], grad]


def local_inverse(rows, twist, small, last):
    re = jnp.concatenate([rows[0].T, rows[1].T], axis=0)
    im = jnp.concatenate([rows[2].T, rows[3].T], axis=0)
    z = product(split(jnp.concatenate([re, im], axis=1)), last)
    outs = [None] * A
    for k in range(A):
        wr, wi = twist[0][k : k + 1], twist[1][k : k + 1]
        zr, zi = z[k * ROWS : (k + 1) * ROWS, :T], z[k * ROWS : (k + 1) * ROWS, T:]
        yr, yi = zr * wr + zi * wi, zi * wr - zr * wi
        for a in range(A):
            c = ROOT[a][k].conjugate()
            term = yr * (c.real * SCALE) - yi * (c.imag * SCALE)
            outs[a] = term if outs[a] is None else outs[a] + term
    g = rows[4].T
    zg = product(split(jnp.concatenate([g[:A], g[A : 2 * A]], axis=1)), last)
    wr, wi = twist
    zr, zi = zg[:, :T], zg[:, T:]
    yr, yi = zr * wr + zi * wi, zi * wr - zr * wi
    grad = 0.0
    for k in range(A):
        grad = grad + (small[0][:, k : k + 1] * yr[k : k + 1] + small[1][:, k : k + 1] * yi[k : k + 1])
    return outs, grad * SCALE


NAMES = ("twist", "small", "fore", "wide", "wide_f", "narrow", "narrow_g", "spread", "gather", "last")
SLOT = 8
USED = 5


def kernel(sig, cot, taps, *refs):
    n = len(NAMES)
    sources, (conv_out, grad_out) = refs[:n], refs[n : n + 2]
    held = dict(zip(NAMES, refs[n + 2 : 2 * n + 2]))
    out1, in1, out2, in2, own, others, load, s1, r1, s2, r2, s3, r3 = refs[2 * n + 2 :]
    me, chan = lax.axis_index("context"), lax.axis_index("chan")

    barrier = pltpu.get_barrier_semaphore()

    def greet(i, c):
        pl.semaphore_signal(
            barrier, inc=1, device_id=(lax.rem(me + i, BLOCKS), chan), device_id_type=MESH
        )
        return c

    lax.fori_loop(1, BLOCKS, greet, 0)
    for i in range(1, CHANS):
        pl.semaphore_signal(
            barrier, inc=1, device_id=(me, lax.rem(chan + i, CHANS)), device_id_type=MESH
        )

    loads = {
        name: pltpu.make_async_copy(source, held[name], load.at[i])
        for i, (name, source) in enumerate(zip(NAMES, sources))
    }
    for copy in loads.values():
        copy.start()

    def table(name):
        loads[name].wait()
        return held[name][...]

    def exchange(source, target, sent, arrived):
        def slot(ref, i):
            return ref.at[pl.ds(pl.multiple_of(i * SLOT, SLOT), USED)]

        def send(i, c):
            peer = lax.rem(me + i, BLOCKS)
            pltpu.make_async_remote_copy(
                src_ref=slot(source, peer),
                dst_ref=slot(target, me),
                send_sem=sent,
                recv_sem=arrived,
                device_id=(peer, chan),
                device_id_type=MESH,
            ).start()
            return c

        lax.fori_loop(1, BLOCKS, send, 0)
        stay = pltpu.make_async_copy(slot(source, me), slot(target, me), sent)
        stay.start()

        whole = source.at[pl.ds(0, BLOCKS * USED)]
        pltpu.make_async_copy(whole, whole, sent).wait()
        part = source.at[pl.ds(0, (BLOCKS - 1) * USED)]
        pltpu.make_async_copy(part, part, arrived).wait()

    def put(ref, rows):
        for i, row in enumerate(rows):
            ref[pl.ds(i, BLOCKS, stride=SLOT), :] = row

    def take(ref):
        return [ref[pl.ds(i, BLOCKS, stride=SLOT), :] for i in range(USED)]

    twist, small = table("twist"), table("small")
    put(
        out1,
        local_forward(
            lambda a: sig[:, a * T : (a + 1) * T],
            lambda a: cot[:, a * T : (a + 1) * T],
            taps[...],
            twist,
            small,
            table("fore"),
        ),
    )
    pl.semaphore_wait(barrier, BLOCKS - 1 + CHANS - 1)
    exchange(out1, in1, s1, r1)
    names = ("wide", "wide_f", "narrow", "narrow_g", "spread", "gather")
    put(out2, middle(take(in1), *[table(name) for name in names]))
    exchange(out2, in2, s2, r2)
    outs, grad = local_inverse(take(in2), held["twist"][...], held["small"][...], table("last"))
    own[...] = grad
    copies = []
    for i in range(1, CHANS):
        copies.append(
            pltpu.make_async_remote_copy(
                src_ref=own,
                dst_ref=others.at[i - 1],
                send_sem=s3.at[i - 1],
                recv_sem=r3.at[i - 1],
                device_id=(me, lax.rem(chan + i, CHANS)),
                device_id_type=MESH,
            )
        )
    for copy in copies:
        copy.start()
    for a in range(A):
        conv_out[:, a * T : (a + 1) * T] = outs[a]
    for copy in copies:
        copy.wait()
    pieces = [own[...]] + [others[i] for i in range(CHANS - 1)]
    total = 0.0
    for g in range(CHANS):
        at = lax.rem(chan - g + CHANS, CHANS)
        piece = pieces[0]
        for i in range(1, CHANS):
            piece = jnp.where(at == i, pieces[i], piece)
        total = total + piece
    grad_out[...] = total


def body(signal, filter_taps, skip_gain, cotangent):
    made = tables()
    consts = [jnp.asarray(made[name]) for name in NAMES]
    whole = pl.BlockSpec(memory_space=pltpu.VMEM)
    conv, grad = pl.pallas_call(
        kernel,
        out_shape=(
            jax.ShapeDtypeStruct((ROWS, LOCAL), F32),
            jax.ShapeDtypeStruct((A, T), F32),
        ),
        in_specs=[whole] * 3 + [pl.BlockSpec(memory_space=pl.ANY)] * len(NAMES),
        out_specs=(whole, whole),
        scratch_shapes=[pltpu.VMEM(c.shape, c.dtype) for c in consts]
        + [pltpu.VMEM((BLOCKS * SLOT, 128), F32)] * 4
        + [pltpu.VMEM((A, T), F32), pltpu.VMEM((CHANS - 1, A, T), F32)]
        + [pltpu.SemaphoreType.DMA((len(NAMES),))]
        + [pltpu.SemaphoreType.DMA] * 4
        + [pltpu.SemaphoreType.DMA((CHANS - 1,))] * 2,
        compiler_params=pltpu.CompilerParams(collective_id=0, has_side_effects=True),
        name="hyena",
    )(signal, cotangent, filter_taps.reshape(A, T), *consts)
    gain = skip_gain[:, None]
    half = ROWS // 2
    return (
        conv[:half] + gain * signal,
        conv[half:] + gain * cotangent,
        grad.reshape(LOCAL),
    )


def solution(mesh):
    return jax.shard_map(
        body,
        mesh=mesh,
        in_specs=(P("chan", "context"), P("context"), P("chan"), P("chan", "context")),
        out_specs=(P("chan", "context"), P("chan", "context"), P("context")),
        check_vma=False,
    )
```

```python
import functools
import math

import jax
import jax.numpy as jnp
import numpy as np
from jax import lax
from jax.experimental import pallas as pl
from jax.experimental.pallas import tpu as pltpu
from jax.sharding import PartitionSpec as P

MESH = pl.DeviceIdType.MESH
F32, BF16 = jnp.float32, jnp.bfloat16
BLOCKS, CHANS = 128, 4
A, T = 8, 128
LOCAL = A * T
PAD = 2 * BLOCKS
ROWS = 32
SCALE = 1.0 / (PAD * LOCAL * math.sqrt(BLOCKS * LOCAL))


def as_real(left):
    return np.block([[left.real, -left.imag], [left.imag, left.real]])


def halves(table):
    high = np.asarray(table, np.float32).astype(BF16)
    low = (table - high.astype(np.float64)).astype(np.float32).astype(BF16)
    return np.stack([high, low])


def tables():
    turn = lambda x: np.exp(-2j * np.pi * x)
    t = np.arange(T)
    ka = np.arange(A)
    near = turn(np.outer(t, t) / T)
    far = turn(np.outer(np.arange(PAD), np.arange(BLOCKS)) / PAD)
    fold = 1 + 1j * turn(np.arange(PAD) / PAD)
    back = far.conj().T
    fore = as_real(near)
    last = as_real(near.conj()).T
    spread = np.zeros((2, 128, A * ROWS))
    gather = np.zeros((A * ROWS, 128))
    for k in range(A):
        spread[:, k, k * ROWS : (k + 1) * ROWS] = 1
        spread[1, k, k * ROWS + ROWS // 2 : (k + 1) * ROWS] = -1
        gather[k * ROWS + ROWS // 2 : (k + 1) * ROWS, k] = 1
    twist = turn(np.outer(4 * ka + 1, t) / (4 * LOCAL))
    small = np.zeros((4, A, 128))
    roots = turn(np.outer(ka, 4 * ka + 1) / 32)
    for i, part in enumerate((roots.real, roots.imag, roots.real.T, roots.imag.T)):
        small[i, :, :A] = part
    return dict(
        fore=halves(fore),
        last=halves(last),
        wide=halves(as_real(far)),
        wide_f=halves(as_real(far * fold[:, None])),
        narrow=halves(as_real(back)),
        narrow_g=halves(as_real(back * fold.conj()[None, :])),
        spread=spread.astype(BF16),
        gather=gather.astype(BF16),
        twist=np.stack([twist.real, twist.imag]).astype(np.float32),
        small=small.astype(np.float32),
    )


ROOT = [[complex(np.exp(-2j * np.pi * a * (4 * k + 1) / 32)) for k in range(A)] for a in range(A)]


def split(x):
    high = x.astype(BF16)
    return high, (x - high.astype(F32)).astype(BF16)


def dot(x, y, dims):
    return lax.dot_general(x, y, (dims, ((), ())), preferred_element_type=F32)


NN = ((1,), (0,))
NT = ((1,), (1,))


def product(left, right, dims=NN):
    (lh, ll), (rh, rl) = left, right
    return dot(lh, rh, dims) + (dot(lh, rl, dims) + dot(ll, rh, dims))


def local_forward(signal, cotangent, taps, twist, small, fore):
    parts = []
    for k in range(A):
        re = im = None
        for a in range(A):
            x = jnp.concatenate([signal(a), cotangent(a)], axis=0)
            c = ROOT[a][k]
            re = x * c.real if re is None else re + x * c.real
            im = x * c.imag if im is None else im + x * c.imag
        wr, wi = twist[0][k : k + 1], twist[1][k : k + 1]
        parts.append(jnp.concatenate([re * wr - im * wi, re * wi + im * wr], axis=1))
    z = split(jnp.concatenate(parts, axis=0))
    out = product(fore, z, NT)
    re = im = 0.0
    for a in range(A):
        x = taps[a : a + 1]
        re = re + small[2][:, a : a + 1] * x
        im = im + small[3][:, a : a + 1] * x
    wr, wi = twist
    re, im = re * wr - im * wi, re * wi + im * wr
    zf = jnp.concatenate(
        [
            jnp.concatenate([re, im], axis=1),
            jnp.concatenate([im, -re], axis=1),
            jnp.zeros((128 - 2 * A, 2 * T), F32),
        ],
        axis=0,
    )
    outf = product((fore[0][:T], fore[1][:T]), split(zf), NT)
    return [out[:T, :128], out[:T, 128:], out[T:, :128], out[T:, 128:], outf]


def along_blocks(rows, wide):
    x = jnp.concatenate(
        [jnp.concatenate(rows[0:2], axis=1), jnp.concatenate(rows[2:4], axis=1)], axis=0
    )
    return product(wide, split(x))


def convolve(v, xf, wide_f, narrow, spread):
    xf = jnp.concatenate([xf, pltpu.roll(xf, 128 - A, 1)], axis=0)
    gh, gl = split(product(wide_f, split(xf)))
    gr = dot(gh[:PAD], spread[0], NN) + dot(gl[:PAD], spread[0], NN)
    gi = dot(gh[PAD:], spread[1], NN) + dot(gl[PAD:], spread[1], NN)
    vr, vi = v[:PAD], v[PAD:]
    p = jnp.concatenate([vr * gr - vi * gi, vr * gi + vi * gr], axis=0)
    w = product(narrow, split(p))
    return [w[:BLOCKS, :128], w[:BLOCKS, 128:], w[BLOCKS:, :128], w[BLOCKS:, 128:]]


def correlate(v, narrow_g, gather):
    vr, vi = v[:PAD], v[PAD:]
    turned = jnp.concatenate(
        [pltpu.roll(v[:, :128], ROWS // 2, 1), pltpu.roll(v[:, 128:], ROWS // 2, 1)], axis=1
    )
    sr, si = turned[:PAD], turned[PAD:]
    qh, ql = split(jnp.concatenate([vr * sr + vi * si, vi * sr - vr * si], axis=0))
    d = dot(qh, gather, NN) + dot(ql, gather, NN)
    e = product(narrow_g, split(d))
    return e[:BLOCKS] + pltpu.roll(e[BLOCKS:], A, 1)


def local_inverse(rows, twist, last):
    re = jnp.concatenate([rows[0].T, rows[1].T], axis=0)
    im = jnp.concatenate([rows[2].T, rows[3].T], axis=0)
    z = product(split(jnp.concatenate([re, im], axis=1)), last)
    outs = [None] * A
    for k in range(A):
        wr, wi = twist[0][k : k + 1], twist[1][k : k + 1]
        zr, zi = z[k * ROWS : (k + 1) * ROWS, :T], z[k * ROWS : (k + 1) * ROWS, T:]
        yr, yi = zr * wr + zi * wi, zi * wr - zr * wi
        for a in range(A):
            c = ROOT[a][k].conjugate()
            term = yr * (c.real * SCALE) - yi * (c.imag * SCALE)
            outs[a] = term if outs[a] is None else outs[a] + term
    return outs


def inverse_taps(row, twist, small, last):
    g = row.T
    zg = product(split(jnp.concatenate([g[:A], g[A : 2 * A]], axis=1)), last)
    wr, wi = twist
    zr, zi = zg[:, :T], zg[:, T:]
    yr, yi = zr * wr + zi * wi, zi * wr - zr * wi
    grad = 0.0
    for k in range(A):
        grad = grad + (small[0][:, k : k + 1] * yr[k : k + 1] + small[1][:, k : k + 1] * yi[k : k + 1])
    return grad * SCALE


NAMES = ("signal", "cotangent", "taps", "gain", "twist", "small", "fore", "wide", "wide_f", "narrow", "narrow_g", "spread", "gather", "last")
SLOT = 8
LIMIT = 60 * 1024 * 1024


def kernel(*refs):
    n = len(NAMES)
    sources, (out_s, out_c, out_f) = refs[:n], refs[n : n + 3]
    held = dict(zip(NAMES, refs[n + 3 : 2 * n + 3]))
    out1, in1, out2, in2, own, others, load, s1, r1, sg, rg, s2, r2, s3, r3 = refs[2 * n + 3 :]
    me, chan = lax.axis_index("context"), lax.axis_index("chan")

    barrier = pltpu.get_barrier_semaphore()

    def greet(i, c):
        pl.semaphore_signal(
            barrier, inc=1, device_id=(lax.rem(me + i, BLOCKS), chan), device_id_type=MESH
        )
        return c

    lax.fori_loop(1, BLOCKS, greet, 0)
    for i in range(1, CHANS):
        pl.semaphore_signal(
            barrier, inc=1, device_id=(me, lax.rem(chan + i, CHANS)), device_id_type=MESH
        )

    loads = {
        name: pltpu.make_async_copy(source, held[name], load.at[i])
        for i, (name, source) in enumerate(zip(NAMES, sources))
    }
    for copy in loads.values():
        copy.start()

    def table(name):
        loads[name].wait()
        return held[name][...]

    def slot(ref, i, first, count):
        return ref.at[pl.ds(pl.multiple_of(i * SLOT, SLOT) + first, count)]

    def start(source, target, sent, arrived, first, count):
        def send(i, c):
            peer = lax.rem(me + i, BLOCKS)
            pltpu.make_async_remote_copy(
                src_ref=slot(source, peer, first, count),
                dst_ref=slot(target, me, first, count),
                send_sem=sent,
                recv_sem=arrived,
                device_id=(peer, chan),
                device_id_type=MESH,
            ).start()
            return c

        pltpu.make_async_copy(
            slot(source, me, first, count), slot(target, me, first, count), sent
        ).start()
        lax.fori_loop(1, BLOCKS, send, 0)

    def finish(source, sent, arrived, count):
        whole = source.at[pl.ds(0, BLOCKS * count)]
        pltpu.make_async_copy(whole, whole, sent).wait()
        part = source.at[pl.ds(0, (BLOCKS - 1) * count)]
        pltpu.make_async_copy(part, part, arrived).wait()

    def put(ref, rows):
        for i, row in enumerate(rows):
            ref[pl.ds(i, BLOCKS, stride=SLOT), :] = row

    def take(ref, first, last):
        return [ref[pl.ds(i, BLOCKS, stride=SLOT), :] for i in range(first, last)]

    for name in ("signal", "cotangent"):
        loads[name].wait()
    sig, cot = held["signal"], held["cotangent"]
    taps = table("taps")
    loads["gain"].wait()
    twist, small = table("twist"), table("small")
    put(
        out1,
        local_forward(
            lambda a: sig[:, a * T : (a + 1) * T],
            lambda a: cot[:, a * T : (a + 1) * T],
            taps,
            twist,
            small,
            table("fore"),
        ),
    )
    for name in ("wide", "wide_f", "narrow", "narrow_g", "spread", "gather", "last"):
        loads[name].wait()
    pl.semaphore_wait(barrier, BLOCKS - 1 + CHANS - 1)
    start(out1, in1, s1, r1, 0, 5)
    finish(out1, s1, r1, 5)

    rows = take(in1, 0, 5)
    v = along_blocks(rows, held["wide"][...])
    out2[pl.ds(4, BLOCKS, stride=SLOT), :] = correlate(
        v, held["narrow_g"][...], held["gather"][...]
    )
    start(out2, in2, sg, rg, 4, 1)
    put(
        out2,
        convolve(v, rows[4], held["wide_f"][...], held["narrow"][...], held["spread"][...]),
    )
    start(out2, in2, s2, r2, 0, 4)

    finish(out2, sg, rg, 1)
    own[...] = inverse_taps(
        take(in2, 4, 5)[0], held["twist"][...], held["small"][...], held["last"][...]
    )
    copies = []
    for i in range(1, CHANS):
        copies.append(
            pltpu.make_async_remote_copy(
                src_ref=own,
                dst_ref=others.at[i - 1],
                send_sem=s3.at[i - 1],
                recv_sem=r3.at[i - 1],
                device_id=(me, lax.rem(chan + i, CHANS)),
                device_id_type=MESH,
            )
        )
    for copy in copies:
        copy.start()

    finish(out2, s2, r2, 4)
    outs = local_inverse(take(in2, 0, 4), held["twist"][...], held["last"][...])
    half = ROWS // 2
    row = lax.broadcasted_iota(jnp.int32, (half, T), 0)
    column = jnp.zeros((half, T), F32)
    for r in range(half):
        column = jnp.where(row == r, held["gain"][r], column)
    for a in range(A):
        at = slice(a * T, (a + 1) * T)
        out_s[:, at] = outs[a][:half] + column * sig[:, at]
        out_c[:, at] = outs[a][half:] + column * cot[:, at]
    for copy in copies:
        copy.wait()
    pieces = [own[...]] + [others[i] for i in range(CHANS - 1)]
    total = 0.0
    for g in range(CHANS):
        at = lax.rem(chan - g + CHANS, CHANS)
        piece = pieces[0]
        for i in range(1, CHANS):
            piece = jnp.where(at == i, pieces[i], piece)
        total = total + piece
    out_f[...] = total


def body(signal, filter_taps, skip_gain, cotangent):
    made = tables()
    consts = [signal, cotangent, filter_taps.reshape(A, T), skip_gain]
    consts += [jnp.asarray(made[name]) for name in NAMES[4:]]
    vmem = pl.BlockSpec(memory_space=pltpu.VMEM)
    hbm = pl.BlockSpec(memory_space=pltpu.HBM)
    block = jax.ShapeDtypeStruct((ROWS // 2, LOCAL), F32)
    line = jax.ShapeDtypeStruct((A, T), F32)
    output, grad_signal, grad_filter = pl.pallas_call(
        kernel,
        out_shape=(block, block, line),
        in_specs=[hbm] * len(NAMES),
        out_specs=(vmem,) * 3,
        scratch_shapes=[
            (pltpu.SMEM if name == "gain" else pltpu.VMEM)(c.shape, c.dtype)
            for name, c in zip(NAMES, consts)
        ]
        + [pltpu.VMEM((BLOCKS * SLOT, 128), F32)] * 4
        + [pltpu.VMEM((A, T), F32), pltpu.VMEM((CHANS - 1, A, T), F32)]
        + [pltpu.SemaphoreType.DMA((len(NAMES),))]
        + [pltpu.SemaphoreType.DMA] * 6
        + [pltpu.SemaphoreType.DMA((CHANS - 1,))] * 2,
        compiler_params=pltpu.CompilerParams(
            collective_id=0, has_side_effects=True, vmem_limit_bytes=LIMIT
        ),
        name="hyena",
    )(*consts)
    return output, grad_signal, grad_filter.reshape(LOCAL)


def solution(mesh):
    return jax.shard_map(
        body,
        mesh=mesh,
        in_specs=(P("chan", "context"), P("context"), P("chan"), P("chan", "context")),
        out_specs=(P("chan", "context"), P("chan", "context"), P("context")),
        check_vma=False,
    )
```

```python
import functools
import math

import jax
import jax.numpy as jnp
import numpy as np
from jax import lax
from jax.experimental import pallas as pl
from jax.experimental.pallas import tpu as pltpu
from jax.sharding import PartitionSpec as P

MESH = pl.DeviceIdType.MESH
F32, BF16 = jnp.float32, jnp.bfloat16
BLOCKS, CHANS = 128, 4
A, T = 8, 128
LOCAL = A * T
PAD = 2 * BLOCKS
ROWS = 32
SCALE = 1.0 / (PAD * LOCAL * math.sqrt(BLOCKS * LOCAL))


def as_real(left):
    return np.block([[left.real, -left.imag], [left.imag, left.real]])


def halves(table):
    high = np.asarray(table, np.float32).astype(BF16)
    low = (table - high.astype(np.float64)).astype(np.float32).astype(BF16)
    return np.stack([high, low])


def tables():
    turn = lambda x: np.exp(-2j * np.pi * x)
    t = np.arange(T)
    ka = np.arange(A)
    near = turn(np.outer(t, t) / T)
    far = turn(np.outer(np.arange(PAD), np.arange(BLOCKS)) / PAD)
    fold = 1 + 1j * turn(np.arange(PAD) / PAD)
    back = far.conj().T
    fore = as_real(near)
    last = as_real(near.conj()).T
    spread = np.zeros((2, 128, A * ROWS))
    gather = np.zeros((A * ROWS, 128))
    for k in range(A):
        spread[:, k, k * ROWS : (k + 1) * ROWS] = 1
        spread[1, k, k * ROWS + ROWS // 2 : (k + 1) * ROWS] = -1
        gather[k * ROWS + ROWS // 2 : (k + 1) * ROWS, k] = 1
    twist = turn(np.outer(4 * ka + 1, t) / (4 * LOCAL))
    small = np.zeros((4, A, 128))
    roots = turn(np.outer(ka, 4 * ka + 1) / 32)
    for i, part in enumerate((roots.real, roots.imag, roots.real.T, roots.imag.T)):
        small[i, :, :A] = part
    return dict(
        fore=halves(fore),
        last=halves(last),
        wide=halves(as_real(far)),
        wide_f=halves(as_real(far * fold[:, None])),
        narrow=halves(as_real(back)),
        narrow_g=halves(as_real(back * fold.conj()[None, :])),
        spread=spread.astype(BF16),
        gather=gather.astype(BF16),
        twist=np.stack([twist.real, twist.imag]).astype(np.float32),
        small=small.astype(np.float32),
    )


ROOT = [[complex(np.exp(-2j * np.pi * a * (4 * k + 1) / 32)) for k in range(A)] for a in range(A)]


def split(x):
    high = x.astype(BF16)
    return high, (x - high.astype(F32)).astype(BF16)


def dot(x, y, dims):
    return lax.dot_general(x, y, (dims, ((), ())), preferred_element_type=F32)


NN = ((1,), (0,))
NT = ((1,), (1,))


def product(left, right, dims=NN):
    (lh, ll), (rh, rl) = left, right
    return dot(lh, rh, dims) + (dot(lh, rl, dims) + dot(ll, rh, dims))


def local_forward(signal, cotangent, taps, twist, small, fore):
    parts = []
    for k in range(A):
        re = im = None
        for a in range(A):
            x = jnp.concatenate([signal(a), cotangent(a)], axis=0)
            c = ROOT[a][k]
            re = x * c.real if re is None else re + x * c.real
            im = x * c.imag if im is None else im + x * c.imag
        wr, wi = twist[0][k : k + 1], twist[1][k : k + 1]
        parts.append(jnp.concatenate([re * wr - im * wi, re * wi + im * wr], axis=1))
    z = split(jnp.concatenate(parts, axis=0))
    out = product(fore, z, NT)
    re = im = 0.0
    for a in range(A):
        x = taps[a : a + 1]
        re = re + small[2][:, a : a + 1] * x
        im = im + small[3][:, a : a + 1] * x
    wr, wi = twist
    re, im = re * wr - im * wi, re * wi + im * wr
    zf = jnp.concatenate(
        [
            jnp.concatenate([re, im], axis=1),
            jnp.concatenate([im, -re], axis=1),
            jnp.zeros((128 - 2 * A, 2 * T), F32),
        ],
        axis=0,
    )
    outf = product((fore[0][:T], fore[1][:T]), split(zf), NT)
    return [out[:T, :128], out[:T, 128:], out[T:, :128], out[T:, 128:], outf]


def along_blocks(rows, wide):
    x = jnp.concatenate(
        [jnp.concatenate(rows[0:2], axis=1), jnp.concatenate(rows[2:4], axis=1)], axis=0
    )
    return product(wide, split(x))


def convolve(v, xf, wide_f, narrow, spread):
    xf = jnp.concatenate([xf, pltpu.roll(xf, 128 - A, 1)], axis=0)
    gh, gl = split(product(wide_f, split(xf)))
    gb = jnp.concatenate([gh, gl], axis=1)
    gr = dot(gb[:PAD], jnp.concatenate([spread[0], spread[0]], axis=0), NN)
    gi = dot(gb[PAD:], jnp.concatenate([spread[1], spread[1]], axis=0), NN)
    vr, vi = v[:PAD], v[PAD:]
    p = jnp.concatenate([vr * gr - vi * gi, vr * gi + vi * gr], axis=0)
    w = product(narrow, split(p))
    return [w[:BLOCKS, :128], w[:BLOCKS, 128:], w[BLOCKS:, :128], w[BLOCKS:, 128:]]


def correlate(v, narrow_g, gather):
    vr, vi = v[:PAD], v[PAD:]
    turned = jnp.concatenate(
        [pltpu.roll(v[:, :128], ROWS // 2, 1), pltpu.roll(v[:, 128:], ROWS // 2, 1)], axis=1
    )
    sr, si = turned[:PAD], turned[PAD:]
    qh, ql = split(jnp.concatenate([vr * sr + vi * si, vi * sr - vr * si], axis=0))
    d = dot(qh, gather, NN) + dot(ql, gather, NN)
    e = product(narrow_g, split(d))
    return e[:BLOCKS] + pltpu.roll(e[BLOCKS:], A, 1)


def local_inverse(rows, twist, last):
    re = jnp.concatenate([rows[0].T, rows[1].T], axis=0)
    im = jnp.concatenate([rows[2].T, rows[3].T], axis=0)
    z = product(split(jnp.concatenate([re, im], axis=1)), last)
    outs = [None] * A
    for k in range(A):
        wr, wi = twist[0][k : k + 1], twist[1][k : k + 1]
        zr, zi = z[k * ROWS : (k + 1) * ROWS, :T], z[k * ROWS : (k + 1) * ROWS, T:]
        yr, yi = zr * wr + zi * wi, zi * wr - zr * wi
        for a in range(A):
            c = ROOT[a][k].conjugate()
            term = yr * (c.real * SCALE) - yi * (c.imag * SCALE)
            outs[a] = term if outs[a] is None else outs[a] + term
    return outs


def inverse_taps(row, twist, small, last):
    g = row.T
    zg = product(split(jnp.concatenate([g[:A], g[A : 2 * A]], axis=1)), last)
    wr, wi = twist
    zr, zi = zg[:, :T], zg[:, T:]
    yr, yi = zr * wr + zi * wi, zi * wr - zr * wi
    grad = 0.0
    for k in range(A):
        grad = grad + (small[0][:, k : k + 1] * yr[k : k + 1] + small[1][:, k : k + 1] * yi[k : k + 1])
    return grad * SCALE


NAMES = ("signal", "cotangent", "taps", "gain", "twist", "small", "fore", "wide", "wide_f", "narrow", "narrow_g", "spread", "gather", "last")
SLOT = 8
GROUP = 7
LIMIT = 60 * 1024 * 1024


def kernel(*refs):
    n = len(NAMES)
    sources, (out_s, out_c, out_f) = refs[:n], refs[n : n + 3]
    held = dict(zip(NAMES, refs[n + 3 : 2 * n + 3]))
    out1, in1, out2, in2, own, others, load, s1, r1, sg, rg, s2, r2, s3, r3 = refs[2 * n + 3 :]
    me, chan = lax.axis_index("context"), lax.axis_index("chan")

    barrier = pltpu.get_barrier_semaphore()

    def each_peer(visit):
        def turn(i, c):
            for j in range(GROUP):
                peer = me + (i * GROUP + j + 1)
                visit(jnp.where(peer >= BLOCKS, peer - BLOCKS, peer))
            return c

        whole = (BLOCKS - 1) // GROUP
        lax.fori_loop(0, whole, turn, 0)
        for j in range(whole * GROUP + 1, BLOCKS):
            peer = me + j
            visit(jnp.where(peer >= BLOCKS, peer - BLOCKS, peer))

    def greet(peer):
        pl.semaphore_signal(barrier, inc=1, device_id=(peer, chan), device_id_type=MESH)

    each_peer(greet)
    for i in range(1, CHANS):
        pl.semaphore_signal(
            barrier, inc=1, device_id=(me, lax.rem(chan + i, CHANS)), device_id_type=MESH
        )

    loads = {
        name: pltpu.make_async_copy(source, held[name], load.at[i])
        for i, (name, source) in enumerate(zip(NAMES, sources))
    }
    for copy in loads.values():
        copy.start()

    def table(name):
        loads[name].wait()
        return held[name][...]

    def slot(ref, i, first, count):
        return ref.at[pl.ds(pl.multiple_of(i * SLOT, SLOT) + first, count)]

    def start(source, target, sent, arrived, first, count):
        def send(peer):
            pltpu.make_async_remote_copy(
                src_ref=slot(source, peer, first, count),
                dst_ref=slot(target, me, first, count),
                send_sem=sent,
                recv_sem=arrived,
                device_id=(peer, chan),
                device_id_type=MESH,
            ).start()

        pltpu.make_async_copy(
            slot(source, me, first, count), slot(target, me, first, count), sent
        ).start()
        each_peer(send)

    def finish(source, sent, arrived, count):
        whole = source.at[pl.ds(0, BLOCKS * count)]
        pltpu.make_async_copy(whole, whole, sent).wait()
        part = source.at[pl.ds(0, (BLOCKS - 1) * count)]
        pltpu.make_async_copy(part, part, arrived).wait()

    def put(ref, rows):
        for i, row in enumerate(rows):
            ref[pl.ds(i, BLOCKS, stride=SLOT), :] = row

    def take(ref, first, last):
        return [ref[pl.ds(i, BLOCKS, stride=SLOT), :] for i in range(first, last)]

    for name in ("signal", "cotangent"):
        loads[name].wait()
    sig, cot = held["signal"], held["cotangent"]
    taps = table("taps")
    loads["gain"].wait()
    twist, small = table("twist"), table("small")
    put(
        out1,
        local_forward(
            lambda a: sig[:, a * T : (a + 1) * T],
            lambda a: cot[:, a * T : (a + 1) * T],
            taps,
            twist,
            small,
            table("fore"),
        ),
    )
    for name in ("wide", "wide_f", "narrow", "narrow_g", "spread", "gather", "last"):
        loads[name].wait()
    pl.semaphore_wait(barrier, BLOCKS - 1 + CHANS - 1)
    start(out1, in1, s1, r1, 0, 5)
    finish(out1, s1, r1, 5)

    rows = take(in1, 0, 5)
    v = along_blocks(rows, held["wide"][...])
    out2[pl.ds(4, BLOCKS, stride=SLOT), :] = correlate(
        v, held["narrow_g"][...], held["gather"][...]
    )
    start(out2, in2, sg, rg, 4, 1)
    put(
        out2,
        convolve(v, rows[4], held["wide_f"][...], held["narrow"][...], held["spread"][...]),
    )
    start(out2, in2, s2, r2, 0, 4)

    finish(out2, sg, rg, 1)
    own[...] = inverse_taps(
        take(in2, 4, 5)[0], held["twist"][...], held["small"][...], held["last"][...]
    )
    copies = []
    for i in range(1, CHANS):
        copies.append(
            pltpu.make_async_remote_copy(
                src_ref=own,
                dst_ref=others.at[i - 1],
                send_sem=s3.at[i - 1],
                recv_sem=r3.at[i - 1],
                device_id=(me, lax.rem(chan + i, CHANS)),
                device_id_type=MESH,
            )
        )
    for copy in copies:
        copy.start()

    finish(out2, s2, r2, 4)
    outs = local_inverse(take(in2, 0, 4), held["twist"][...], held["last"][...])
    half = ROWS // 2
    row = lax.broadcasted_iota(jnp.int32, (half, T), 0)
    column = jnp.zeros((half, T), F32)
    for r in range(half):
        column = jnp.where(row == r, held["gain"][r], column)
    for a in range(A):
        at = slice(a * T, (a + 1) * T)
        out_s[:, at] = outs[a][:half] + column * sig[:, at]
        out_c[:, at] = outs[a][half:] + column * cot[:, at]
    for copy in copies:
        copy.wait()
    pieces = [own[...]] + [others[i] for i in range(CHANS - 1)]
    total = 0.0
    for g in range(CHANS):
        at = lax.rem(chan - g + CHANS, CHANS)
        piece = pieces[0]
        for i in range(1, CHANS):
            piece = jnp.where(at == i, pieces[i], piece)
        total = total + piece
    out_f[...] = total


def hand_over(*refs):
    ins = [pltpu.make_async_copy(refs[i], refs[6 + i], refs[9].at[i]) for i in range(3)]
    outs = [pltpu.make_async_copy(refs[6 + i], refs[3 + i], refs[10].at[i]) for i in range(3)]
    for copy in ins:
        copy.start()
    for get, put in zip(ins, outs):
        get.wait()
        put.start()
    for copy in outs:
        copy.wait()


def body(signal, filter_taps, skip_gain, cotangent):
    made = tables()
    consts = [signal, cotangent, filter_taps.reshape(A, T), skip_gain]
    consts += [jnp.asarray(made[name]) for name in NAMES[4:]]
    vmem = pl.BlockSpec(memory_space=pltpu.VMEM)
    hbm = pl.BlockSpec(memory_space=pltpu.HBM)
    block = jax.ShapeDtypeStruct((ROWS // 2, LOCAL), F32)
    line = jax.ShapeDtypeStruct((A, T), F32)
    results = pl.pallas_call(
        kernel,
        out_shape=(block, block, line),
        in_specs=[hbm] * len(NAMES),
        out_specs=(vmem,) * 3,
        scratch_shapes=[
            (pltpu.SMEM if name == "gain" else pltpu.VMEM)(c.shape, c.dtype)
            for name, c in zip(NAMES, consts)
        ]
        + [pltpu.VMEM((BLOCKS * SLOT, 128), F32)] * 4
        + [pltpu.VMEM((A, T), F32), pltpu.VMEM((CHANS - 1, A, T), F32)]
        + [pltpu.SemaphoreType.DMA((len(NAMES),))]
        + [pltpu.SemaphoreType.DMA] * 6
        + [pltpu.SemaphoreType.DMA((CHANS - 1,))] * 2,
        compiler_params=pltpu.CompilerParams(
            collective_id=0, has_side_effects=True, vmem_limit_bytes=LIMIT
        ),
        name="hyena",
    )(*consts)
    output, grad_signal, grad_filter = pl.pallas_call(
        hand_over,
        out_shape=(block, block, line),
        in_specs=[hbm] * 3,
        out_specs=(hbm,) * 3,
        scratch_shapes=[pltpu.VMEM(out.shape, F32) for out in (block, block, line)]
        + [pltpu.SemaphoreType.DMA((3,))] * 2,
        compiler_params=pltpu.CompilerParams(vmem_limit_bytes=LIMIT),
        name="hand_over",
    )(*results)
    return output, grad_signal, grad_filter.reshape(LOCAL)


def solution(mesh):
    return jax.shard_map(
        body,
        mesh=mesh,
        in_specs=(P("chan", "context"), P("context"), P("chan"), P("chan", "context")),
        out_specs=(P("chan", "context"), P("chan", "context"), P("context")),
        check_vma=False,
    )
```

```python
import functools
import math

import jax
import jax.numpy as jnp
import numpy as np
from jax import lax
from jax.experimental import pallas as pl
from jax.experimental.pallas import tpu as pltpu
from jax.sharding import PartitionSpec as P

MESH = pl.DeviceIdType.MESH
F32, BF16 = jnp.float32, jnp.bfloat16
BLOCKS, CHANS = 128, 4
A, T = 8, 128
LOCAL = A * T
PAD = 2 * BLOCKS
ROWS = 32
SCALE = 1.0 / (PAD * LOCAL * math.sqrt(BLOCKS * LOCAL))


def as_real(left):
    return np.block([[left.real, -left.imag], [left.imag, left.real]])


def halves(table):
    high = np.asarray(table, np.float32).astype(BF16)
    low = (table - high.astype(np.float64)).astype(np.float32).astype(BF16)
    return np.stack([high, low])


def tables():
    turn = lambda x: np.exp(-2j * np.pi * x)
    t = np.arange(T)
    ka = np.arange(A)
    near = turn(np.outer(t, t) / T)
    far = turn(np.outer(np.arange(PAD), np.arange(BLOCKS)) / PAD)
    fold = 1 + 1j * turn(np.arange(PAD) / PAD)
    back = far.conj().T
    fore = as_real(near)
    last = as_real(near.conj()).T
    spread = np.zeros((2, 128, A * ROWS))
    gather = np.zeros((A * ROWS, 128))
    for k in range(A):
        spread[:, k, k * ROWS : (k + 1) * ROWS] = 1
        spread[1, k, k * ROWS + ROWS // 2 : (k + 1) * ROWS] = -1
        gather[k * ROWS + ROWS // 2 : (k + 1) * ROWS, k] = 1
    twist = turn(np.outer(4 * ka + 1, t) / (4 * LOCAL))
    small = np.zeros((4, A, 128))
    roots = turn(np.outer(ka, 4 * ka + 1) / 32)
    for i, part in enumerate((roots.real, roots.imag, roots.real.T, roots.imag.T)):
        small[i, :, :A] = part
    return dict(
        fore=halves(fore),
        last=halves(last),
        wide=halves(as_real(far)),
        wide_f=halves(as_real(far * fold[:, None])),
        narrow=halves(as_real(back)),
        narrow_g=halves(as_real(back * fold.conj()[None, :])),
        spread=spread.astype(BF16),
        gather=gather.astype(BF16),
        twist=np.stack([twist.real, twist.imag]).astype(np.float32),
        small=small.astype(np.float32),
    )


ROOT = [[complex(np.exp(-2j * np.pi * a * (4 * k + 1) / 32)) for k in range(A)] for a in range(A)]


def split(x):
    high = x.astype(BF16)
    return high, (x - high.astype(F32)).astype(BF16)


def dot(x, y, dims):
    return lax.dot_general(x, y, (dims, ((), ())), preferred_element_type=F32)


NN = ((1,), (0,))
NT = ((1,), (1,))


def product(left, right, dims=NN):
    (lh, ll), (rh, rl) = left, right
    return dot(lh, rh, dims) + (dot(lh, rl, dims) + dot(ll, rh, dims))


def local_forward(signal, cotangent, taps, twist, small, fore):
    parts = []
    for k in range(A):
        re = im = None
        for a in range(A):
            x = jnp.concatenate([signal(a), cotangent(a)], axis=0)
            c = ROOT[a][k]
            re = x * c.real if re is None else re + x * c.real
            im = x * c.imag if im is None else im + x * c.imag
        wr, wi = twist[0][k : k + 1], twist[1][k : k + 1]
        parts.append(jnp.concatenate([re * wr - im * wi, re * wi + im * wr], axis=1))
    z = split(jnp.concatenate(parts, axis=0))
    out = product(fore, z, NT)
    re = im = 0.0
    for a in range(A):
        x = taps[a : a + 1]
        re = re + small[2][:, a : a + 1] * x
        im = im + small[3][:, a : a + 1] * x
    wr, wi = twist
    re, im = re * wr - im * wi, re * wi + im * wr
    zf = jnp.concatenate(
        [
            jnp.concatenate([re, im], axis=1),
            jnp.concatenate([im, -re], axis=1),
            jnp.zeros((128 - 2 * A, 2 * T), F32),
        ],
        axis=0,
    )
    outf = product((fore[0][:T], fore[1][:T]), split(zf), NT)
    return [out[:T, :128], out[:T, 128:], out[T:, :128], out[T:, 128:], outf]


def along_blocks(rows, wide):
    x = jnp.concatenate(
        [jnp.concatenate(rows[0:2], axis=1), jnp.concatenate(rows[2:4], axis=1)], axis=0
    )
    return product(wide, split(x))


def convolve(v, xf, wide_f, narrow, spread):
    xf = jnp.concatenate([xf, pltpu.roll(xf, 128 - A, 1)], axis=0)
    gh, gl = split(product(wide_f, split(xf)))
    gb = jnp.concatenate([gh, gl], axis=1)
    gr = dot(gb[:PAD], jnp.concatenate([spread[0], spread[0]], axis=0), NN)
    gi = dot(gb[PAD:], jnp.concatenate([spread[1], spread[1]], axis=0), NN)
    vr, vi = v[:PAD], v[PAD:]
    p = jnp.concatenate([vr * gr - vi * gi, vr * gi + vi * gr], axis=0)
    w = product(narrow, split(p))
    return [w[:BLOCKS, :128], w[:BLOCKS, 128:], w[BLOCKS:, :128], w[BLOCKS:, 128:]]


def correlate(v, narrow_g, gather):
    vr, vi = v[:PAD], v[PAD:]
    turned = jnp.concatenate(
        [pltpu.roll(v[:, :128], ROWS // 2, 1), pltpu.roll(v[:, 128:], ROWS // 2, 1)], axis=1
    )
    sr, si = turned[:PAD], turned[PAD:]
    qh, ql = split(jnp.concatenate([vr * sr + vi * si, vi * sr - vr * si], axis=0))
    d = dot(qh, gather, NN) + dot(ql, gather, NN)
    e = product(narrow_g, split(d))
    return e[:BLOCKS] + pltpu.roll(e[BLOCKS:], A, 1)


def local_inverse(rows, twist, last):
    re = jnp.concatenate([rows[0].T, rows[1].T], axis=0)
    im = jnp.concatenate([rows[2].T, rows[3].T], axis=0)
    z = product(split(jnp.concatenate([re, im], axis=1)), last)
    outs = [None] * A
    for k in range(A):
        wr, wi = twist[0][k : k + 1], twist[1][k : k + 1]
        zr, zi = z[k * ROWS : (k + 1) * ROWS, :T], z[k * ROWS : (k + 1) * ROWS, T:]
        yr, yi = zr * wr + zi * wi, zi * wr - zr * wi
        for a in range(A):
            c = ROOT[a][k].conjugate()
            term = yr * (c.real * SCALE) - yi * (c.imag * SCALE)
            outs[a] = term if outs[a] is None else outs[a] + term
    return outs


def inverse_taps(row, twist, small, last):
    g = row.T
    zg = product(split(jnp.concatenate([g[:A], g[A : 2 * A]], axis=1)), last)
    wr, wi = twist
    zr, zi = zg[:, :T], zg[:, T:]
    yr, yi = zr * wr + zi * wi, zi * wr - zr * wi
    grad = 0.0
    for k in range(A):
        grad = grad + (small[0][:, k : k + 1] * yr[k : k + 1] + small[1][:, k : k + 1] * yi[k : k + 1])
    return grad * SCALE


NAMES = ("signal", "cotangent", "taps", "gain", "twist", "small", "fore", "wide", "wide_f", "narrow", "narrow_g", "spread", "gather", "last")
SLOT = 8
GROUP = 7
LIMIT = 60 * 1024 * 1024


def kernel(*refs):
    n = len(NAMES)
    sources, results = refs[:n], refs[n : n + 3]
    held = dict(zip(NAMES, refs[n + 3 : 2 * n + 3]))
    out1, in1, out2, in2, own, others, load, s1, r1, sg, rg, s2, r2, s3, r3, out_s, out_c, out_f, leave = refs[2 * n + 3 :]
    me, chan = lax.axis_index("context"), lax.axis_index("chan")

    barrier = pltpu.get_barrier_semaphore()

    def each_peer(visit):
        def turn(i, c):
            for j in range(GROUP):
                peer = me + (i * GROUP + j + 1)
                visit(jnp.where(peer >= BLOCKS, peer - BLOCKS, peer))
            return c

        whole = (BLOCKS - 1) // GROUP
        lax.fori_loop(0, whole, turn, 0)
        for j in range(whole * GROUP + 1, BLOCKS):
            peer = me + j
            visit(jnp.where(peer >= BLOCKS, peer - BLOCKS, peer))

    def greet(peer):
        pl.semaphore_signal(barrier, inc=1, device_id=(peer, chan), device_id_type=MESH)

    each_peer(greet)
    for i in range(1, CHANS):
        pl.semaphore_signal(
            barrier, inc=1, device_id=(me, lax.rem(chan + i, CHANS)), device_id_type=MESH
        )

    loads = {
        name: pltpu.make_async_copy(source, held[name], load.at[i])
        for i, (name, source) in enumerate(zip(NAMES, sources))
    }
    for copy in loads.values():
        copy.start()

    def table(name):
        loads[name].wait()
        return held[name][...]

    def slot(ref, i, first, count):
        return ref.at[pl.ds(pl.multiple_of(i * SLOT, SLOT) + first, count)]

    def start(source, target, sent, arrived, first, count):
        def send(peer):
            pltpu.make_async_remote_copy(
                src_ref=slot(source, peer, first, count),
                dst_ref=slot(target, me, first, count),
                send_sem=sent,
                recv_sem=arrived,
                device_id=(peer, chan),
                device_id_type=MESH,
            ).start()

        pltpu.make_async_copy(
            slot(source, me, first, count), slot(target, me, first, count), sent
        ).start()
        each_peer(send)

    def finish(source, sent, arrived, count):
        whole = source.at[pl.ds(0, BLOCKS * count)]
        pltpu.make_async_copy(whole, whole, sent).wait()
        part = source.at[pl.ds(0, (BLOCKS - 1) * count)]
        pltpu.make_async_copy(part, part, arrived).wait()

    def put(ref, rows):
        for i, row in enumerate(rows):
            ref[pl.ds(i, BLOCKS, stride=SLOT), :] = row

    def take(ref, first, last):
        return [ref[pl.ds(i, BLOCKS, stride=SLOT), :] for i in range(first, last)]

    for name in ("signal", "cotangent"):
        loads[name].wait()
    sig, cot = held["signal"], held["cotangent"]
    taps = table("taps")
    loads["gain"].wait()
    twist, small = table("twist"), table("small")
    put(
        out1,
        local_forward(
            lambda a: sig[:, a * T : (a + 1) * T],
            lambda a: cot[:, a * T : (a + 1) * T],
            taps,
            twist,
            small,
            table("fore"),
        ),
    )
    for name in ("wide", "wide_f", "narrow", "narrow_g", "spread", "gather", "last"):
        loads[name].wait()
    pl.semaphore_wait(barrier, BLOCKS - 1 + CHANS - 1)
    start(out1, in1, s1, r1, 0, 5)
    finish(out1, s1, r1, 5)

    rows = take(in1, 0, 5)
    v = along_blocks(rows, held["wide"][...])
    out2[pl.ds(4, BLOCKS, stride=SLOT), :] = correlate(
        v, held["narrow_g"][...], held["gather"][...]
    )
    start(out2, in2, sg, rg, 4, 1)
    put(
        out2,
        convolve(v, rows[4], held["wide_f"][...], held["narrow"][...], held["spread"][...]),
    )
    start(out2, in2, s2, r2, 0, 4)

    finish(out2, sg, rg, 1)
    own[...] = inverse_taps(
        take(in2, 4, 5)[0], held["twist"][...], held["small"][...], held["last"][...]
    )
    copies = []
    for i in range(1, CHANS):
        copies.append(
            pltpu.make_async_remote_copy(
                src_ref=own,
                dst_ref=others.at[i - 1],
                send_sem=s3.at[i - 1],
                recv_sem=r3.at[i - 1],
                device_id=(me, lax.rem(chan + i, CHANS)),
                device_id_type=MESH,
            )
        )
    for copy in copies:
        copy.start()

    finish(out2, s2, r2, 4)
    outs = local_inverse(take(in2, 0, 4), held["twist"][...], held["last"][...])
    half = ROWS // 2
    row = lax.broadcasted_iota(jnp.int32, (half, T), 0)
    column = jnp.zeros((half, T), F32)
    for r in range(half):
        column = jnp.where(row == r, held["gain"][r], column)
    for a in range(A):
        at = slice(a * T, (a + 1) * T)
        out_s[:, at] = outs[a][:half] + column * sig[:, at]
        out_c[:, at] = outs[a][half:] + column * cot[:, at]
    leaves = [
        pltpu.make_async_copy(made, result, leave.at[i])
        for i, (made, result) in enumerate(zip((out_s, out_c, out_f), results))
    ]
    leaves[0].start()
    leaves[1].start()
    for copy in copies:
        copy.wait()
    pieces = [own[...]] + [others[i] for i in range(CHANS - 1)]
    total = 0.0
    for g in range(CHANS):
        at = lax.rem(chan - g + CHANS, CHANS)
        piece = pieces[0]
        for i in range(1, CHANS):
            piece = jnp.where(at == i, pieces[i], piece)
        total = total + piece
    out_f[...] = total
    leaves[2].start()
    for copy in leaves:
        copy.wait()


def hand_over(*refs):
    ins = [pltpu.make_async_copy(refs[i], refs[6 + i], refs[9].at[i]) for i in range(3)]
    outs = [pltpu.make_async_copy(refs[6 + i], refs[3 + i], refs[10].at[i]) for i in range(3)]
    for copy in ins:
        copy.start()
    for get, put in zip(ins, outs):
        get.wait()
        put.start()
    for copy in outs:
        copy.wait()


def body(signal, filter_taps, skip_gain, cotangent):
    made = tables()
    consts = [signal, cotangent, filter_taps.reshape(A, T), skip_gain]
    consts += [jnp.asarray(made[name]) for name in NAMES[4:]]
    hbm = pl.BlockSpec(memory_space=pltpu.HBM)
    block = jax.ShapeDtypeStruct((ROWS // 2, LOCAL), F32)
    line = jax.ShapeDtypeStruct((A, T), F32)
    results = pl.pallas_call(
        kernel,
        out_shape=(block, block, line),
        in_specs=[hbm] * len(NAMES),
        out_specs=(hbm,) * 3,
        scratch_shapes=[
            (pltpu.SMEM if name == "gain" else pltpu.VMEM)(c.shape, c.dtype)
            for name, c in zip(NAMES, consts)
        ]
        + [pltpu.VMEM((BLOCKS * SLOT, 128), F32)] * 4
        + [pltpu.VMEM((A, T), F32), pltpu.VMEM((CHANS - 1, A, T), F32)]
        + [pltpu.SemaphoreType.DMA((len(NAMES),))]
        + [pltpu.SemaphoreType.DMA] * 6
        + [pltpu.SemaphoreType.DMA((CHANS - 1,))] * 2
        + [pltpu.VMEM(out.shape, F32) for out in (block, block, line)]
        + [pltpu.SemaphoreType.DMA((3,))],
        compiler_params=pltpu.CompilerParams(
            collective_id=0, has_side_effects=True, vmem_limit_bytes=LIMIT
        ),
        name="hyena",
    )(*consts)
    output, grad_signal, grad_filter = pl.pallas_call(
        hand_over,
        out_shape=(block, block, line),
        in_specs=[hbm] * 3,
        out_specs=(hbm,) * 3,
        scratch_shapes=[pltpu.VMEM(out.shape, F32) for out in (block, block, line)]
        + [pltpu.SemaphoreType.DMA((3,))] * 2,
        compiler_params=pltpu.CompilerParams(vmem_limit_bytes=LIMIT),
        name="hand_over",
    )(*results)
    return output, grad_signal, grad_filter.reshape(LOCAL)


def solution(mesh):
    return jax.shard_map(
        body,
        mesh=mesh,
        in_specs=(P("chan", "context"), P("context"), P("chan"), P("chan", "context")),
        out_specs=(P("chan", "context"), P("chan", "context"), P("context")),
        check_vma=False,
    )
```
